32 devices in a mesh: pipe: 2 (over x), dp: 4 (over y, core), tensor: 4 (over z).
Axes of the slice: x: 2, y: 2, z: 4, core: 2. Of those that a mesh axis runs over, the one named last changes fastest.
Arguments:
- inputs: bfloat16 [4, 1024, 1024], P(None, ('dp', 'tensor')), may hold values from -6 to 6
- segments: int32 [4, 1024], P(None, 'dp'), may hold values from 0 to 7, never falling along the last dimension, each value on 1 to 256 neighbouring positions
- cotangent: bfloat16 [4, 1024, 1024], P(None, ('dp', 'tensor')), may hold values from -6 to 6
- w_qkv: bfloat16 [2, 1024, 3, 1024], P('pipe', 'dp', None, 'tensor'), may hold values from -0.1875 to 0.1875
- w_o: bfloat16 [2, 1024, 1024], P('pipe', 'tensor', 'dp'), may hold values from -1.5 to 1.5
- w_in: bfloat16 [2, 1024, 4096], P('pipe', 'dp', 'tensor'), may hold values from -0.1875 to 0.1875
- w_out: bfloat16 [2, 4096, 1024], P('pipe', 'tensor', 'dp'), may hold values from -0.09375 to 0.09375
- ln_gains: float32 [2, 2, 1024], P('pipe'), may hold values from 0.1 to 1.9
- model_biases: float32 [2, 6, 1024], P('pipe'), may hold values from -1 to 1
- hidden_bias: float32 [2, 4096], P('pipe'), may hold values from -2.5 to 2.5
Outputs:
- section_outputs: bfloat16 [2, 4, 1024, 1024], P('pipe', None, ('dp', 'tensor'))
- input_grads: bfloat16 [2, 4, 1024, 1024], P('pipe', None, ('dp', 'tensor'))
- grad_qkv: float32 [2, 1024, 3, 1024], P('pipe', 'dp', None, 'tensor')
- grad_o: float32 [2, 1024, 1024], P('pipe', 'tensor', 'dp')
- grad_in: float32 [2, 1024, 4096], P('pipe', 'dp', 'tensor')
- grad_out: float32 [2, 4096, 1024], P('pipe', 'tensor', 'dp')
- grad_gains: float32 [2, 2, 1024], P('pipe', None, ('dp', 'tensor'))
- grad_biases: float32 [2, 6, 1024], P('pipe', None, ('dp', 'tensor'))
- grad_hidden_bias: float32 [2, 4096], P('pipe', ('dp', 'tensor'))
The draws below stay inside these ranges and needn't reach their ends.
Inputs may be any that keep to these rules, and one draw needn't show every extreme that they name: `segments`: segment numbers never fall along a micro-batch's 1024 tokens; a segment holds 1 to 256 tokens and some segment holds exactly 256.
All inputs are finite; a program needn't handle non-finite values.
Results may differ from the reference program's by a relative error of at most 0.028.
Values may be sent and summed in bfloat16 or wider, within the bound.
No kernel may reach another device: no remote copies, remote signals or barrier semaphores. Data moves between devices by JAX's collectives and lax.ppermute only.
A program may use at most 128 MiB of HBM per device.

```python
import math
import jax
import jax.numpy as jnp
import numpy as np
from jax import lax

D = 1024
HEADS = 16
FF = 4096
MICRO = 4
HEAD_DIM = 64
SECTIONS = 2
SEQ = 256
TOKENS_MB = 1024
N_DP = 4


def shard_levels(key, shape, cuts, least, high):
    factor_of = 1.0
    for position, parts in cuts:
        steps = jax.random.uniform(jax.random.fold_in(jax.random.fold_in(key, 6), position), (parts,), jnp.float32, least / len(cuts), high / len(cuts))
        factor_of = factor_of * jnp.repeat(jnp.exp(steps), shape[position] // parts).reshape((-1,) + (1,) * (len(shape) - 1 - position))
    return factor_of


def split_up(count, total, bound, skew):
    loads = [(1 << 20) // math.isqrt(standing ** skew) + 1 for standing in range(2, count + 1)]
    surplus, given = total - bound - (count - 1), [1] * (count - 1)
    while surplus > 0:
        free = [i for i in range(count - 1) if given[i] < bound]
        pool, left = sum([loads[i] for i in free]), surplus
        for i in free:
            more = min(bound - given[i], max(1, left * loads[i] // pool), surplus)
            given[i] = given[i] + more
            surplus = surplus - more
    return np.array([bound] + given)


def uneven(own_key, count, total, most, slope):
    if count == 2:
        one = jax.random.randint(own_key, (), max(1, total - most), min(most, total - 1) + 1)
        return jnp.stack([one, total - one])
    lengths = jnp.asarray(split_up(count, total, most, slope), jnp.int32)
    pairs = (count - 1) // 2
    donor, taker = lengths[1:1 + 2 * pairs:2], lengths[2:2 + 2 * pairs:2]
    slack = jnp.minimum(donor - 1, most - taker)
    moved = jax.random.randint(jax.random.fold_in(own_key, 1), (pairs,), 0, 1 << 20) % (slack + 1)
    lengths = lengths.at[1:1 + 2 * pairs:2].set(donor - moved).at[2:2 + 2 * pairs:2].set(taker + moved)
    return lengths[jax.random.permutation(jax.random.fold_in(own_key, 2), count)]


def normal_values(stream_key, dims, width, reach, shards=(), kind=jnp.bfloat16):
    values = jax.random.normal(stream_key, dims, jnp.float32) * width
    if len(shards) > 0:
        values = shard_levels(stream_key, dims, shards, -0.22, 0.18) * values
    return jnp.clip(values, min=-reach, max=reach).astype(kind)


def setup_inputs(seed: int = 0) -> dict:
    keys = jax.random.split(jax.random.key(seed), 11)
    inputs = normal_values(keys[0], (MICRO, TOKENS_MB, D), 1.0, 6.0, ((1, 16),))
    segments = jax.vmap(lambda own: jnp.searchsorted(jnp.cumsum(uneven(own, 2 * TOKENS_MB // SEQ, TOKENS_MB, SEQ, 1)), jnp.arange(TOKENS_MB), side="right"))(jax.random.split(keys[1], MICRO)).reshape((MICRO, TOKENS_MB)).astype(jnp.int32)
    cotangent = normal_values(keys[2], (MICRO, TOKENS_MB, D), 1.0, 6.0, ((1, 16),))
    w_qkv = normal_values(keys[3], (SECTIONS, D, 3, D), D ** -0.5, 0.1875, ((0, 2), (1, 4), (3, 4)))
    w_o = normal_values(keys[4], (SECTIONS, D, D), (D // 64) ** -0.5, 1.5, ((0, 2), (1, 4), (2, 4)))
    w_in = normal_values(keys[5], (SECTIONS, D, FF), D ** -0.5, 0.1875, ((0, 2), (1, 4), (2, 4)))
    w_out = normal_values(keys[6], (SECTIONS, FF, D), FF ** -0.5, 0.09375, ((0, 2), (1, 4), (2, 4)))
    ln_gains = jnp.clip(1.0 + 0.18 * jax.random.normal(keys[7], (SECTIONS, 2, D), jnp.float32), 0.1, 1.9)
    model_biases = normal_values(keys[8], (SECTIONS, 6, D), 0.2, 1.0, ((0, 2),), jnp.float32)
    hidden_bias = normal_values(keys[9], (SECTIONS, FF), 0.5, 2.5, ((0, 2),), jnp.float32)
    return dict(inputs=inputs, segments=segments, cotangent=cotangent, w_qkv=w_qkv, w_o=w_o, w_in=w_in, w_out=w_out, ln_gains=ln_gains, model_biases=model_biases, hidden_bias=hidden_bias)


@jax.custom_vjp
def low(v):
    return lax.optimization_barrier(v.astype(jnp.bfloat16)).astype(jnp.float32)

@jax.custom_vjp
def low_back(v):
    return v

def low_keep(v):
    return (low(v), None)

def low_pass(kept, grad):
    return (grad,)

def back_keep(v):
    return (v, None)

def back_low(kept, grad):
    return (low(grad),)
low.defvjp(low_keep, low_pass)
low_back.defvjp(back_keep, back_low)
HIGHEST = lax.Precision.HIGHEST
NORM_EPS = 1e-12
MASKED = -1000000000.0

def layer_norm(values, gain_row, shift_row):
    center = values - lax.optimization_barrier(jnp.mean(values, axis=-1, keepdims=True))
    spread = lax.optimization_barrier(jnp.mean(center * center, axis=-1, keepdims=True))
    return center * lax.rsqrt(spread + NORM_EPS) * gain_row + shift_row

def attention(queries, key_rows, value_rows, labels):
    row_count = queries.shape[0]
    seq_count = row_count // SEQ
    queries = queries.reshape(seq_count, SEQ, HEADS, HEAD_DIM)
    key_rows = key_rows.reshape(seq_count, SEQ, HEADS, HEAD_DIM)
    value_rows = value_rows.reshape(seq_count, SEQ, HEADS, HEAD_DIM)
    scores = jnp.einsum('nqhe,nkhe->nhqk', queries, key_rows, precision=HIGHEST) * HEAD_DIM ** (-0.5)
    scores = low_back(scores)
    grouped = labels.reshape(seq_count, SEQ)
    allowed = grouped[:, None, :, None] == grouped[:, None, None, :]
    scores = jnp.where(allowed, scores, MASKED)
    weights = low(jax.nn.softmax(scores, axis=-1))
    context = jnp.einsum('nhqk,nkhe->nqhe', weights, value_rows, precision=HIGHEST)
    return context.reshape(row_count, HEADS * HEAD_DIM)

def block_layer(source_rows, labels, w_qkv, w_o, w_in, w_out, gains, biases, hidden_bias):
    projected = jnp.einsum('rd,dcn->rcn', source_rows, w_qkv, precision=HIGHEST)
    queries = low_back(low(projected[:, 0] + biases[0]))
    key_rows = low_back(low(projected[:, 1]))
    value_rows = low_back(low(projected[:, 2] + biases[1]))
    context = low_back(low(attention(queries, key_rows, value_rows, labels)))
    mixed_rows = low_back(jnp.dot(context, w_o, precision=HIGHEST))
    normed = layer_norm(source_rows + mixed_rows + biases[2], gains[0], biases[3])
    hidden = low_back(jnp.dot(low(normed), w_in, precision=HIGHEST) + hidden_bias)
    active = low(jax.nn.gelu(hidden, approximate=False))
    branch = low_back(jnp.dot(active, w_out, precision=HIGHEST))
    return layer_norm(normed + branch + biases[4], gains[1], biases[5])

def network(source_rows, probe_rows, w_qkv, w_o, w_in, w_out, ln_gains, model_biases, hidden_bias, labels):
    middle = block_layer(source_rows, labels, w_qkv[0], w_o[0], w_in[0], w_out[0], ln_gains[0], model_biases[0], hidden_bias[0])
    passed = low_back(low(middle)) + probe_rows
    final_rows = block_layer(passed, labels, w_qkv[1], w_o[1], w_in[1], w_out[1], ln_gains[1], model_biases[1], hidden_bias[1])
    return (low(final_rows), low(middle))

def reference(inputs, segments, cotangent, w_qkv, w_o, w_in, w_out, ln_gains, model_biases, hidden_bias):
    params = tuple((member.astype(jnp.float32) for member in (w_qkv, w_o, w_in, w_out, ln_gains, model_biases, hidden_bias)))
    block_rows = TOKENS_MB // N_DP
    block_count = MICRO * N_DP
    source = inputs.astype(jnp.float32).reshape(block_count, block_rows, D)
    upstream = cotangent.astype(jnp.float32).reshape(block_count, block_rows, D)
    labels = segments.reshape(block_count, block_rows)
    zero_grads = tuple((jnp.zeros(member.shape, jnp.float32) for member in params))

    def one_block(totals, pieces):
        source_rows, grad_rows, label_rows = pieces
        probe_rows = jnp.zeros(source_rows.shape, jnp.float32)

        def wrapped(rows_in, probe_in, *weights):
            return network(rows_in, probe_in, *weights, label_rows)
        final_rows, backward_fn, middle = jax.vjp(wrapped, source_rows, probe_rows, *params, has_aux=True)
        grad_parts = backward_fn(grad_rows)
        totals = tuple((first_item + second_item for first_item, second_item in zip(totals, grad_parts[2:])))
        return (totals, (middle, final_rows, grad_parts[0], grad_parts[1]))
    totals, outputs = lax.scan(one_block, zero_grads, (source, upstream, labels))
    middle, final_rows, grad_first, grad_second = outputs
    shape_out = (MICRO, TOKENS_MB, D)
    section_outputs = jnp.stack([middle.reshape(shape_out), final_rows.reshape(shape_out)]).astype(jnp.bfloat16)
    input_grads = jnp.stack([grad_first.reshape(shape_out), grad_second.reshape(shape_out)]).astype(jnp.bfloat16)
    return (section_outputs, input_grads, totals[0], totals[1], totals[2], totals[3], totals[4], totals[5], totals[6])
```

```python
import jax
import jax.numpy as jnp
from jax import lax
from jax.sharding import PartitionSpec as P

HEAD_DIM = 64
NORM_EPS = 1e-12
MASKED = -1000000000.0
ROOT_HALF = 0.7071067811865476
INV_ROOT_TWOPI = 0.3989422804014327
LOW = jnp.bfloat16


def swapped(block, axis, bit):
    size = lax.axis_size(axis)
    return lax.ppermute(block, axis, [(i, i ^ bit) for i in range(size)])


def halve_sum(stack, axis, dim, kind):
    size = lax.axis_size(axis)
    own = lax.axis_index(axis)
    bit = 1
    while bit < size:
        count = stack.shape[dim]
        split = stack.reshape(stack.shape[:dim] + (count // 2, 2) + stack.shape[dim + 1 :])
        side = (own // bit) % 2
        kept = lax.dynamic_index_in_dim(split, side, dim + 1, keepdims=False)
        given = lax.dynamic_index_in_dim(split, 1 - side, dim + 1, keepdims=False)
        came = swapped(given, axis, bit)
        stack = (kept.astype(jnp.float32) + came.astype(jnp.float32)).astype(kind)
        bit *= 2
    return lax.squeeze(stack, (dim,))


def dot_rows(left_side, right_side):
    return lax.dot_general(
        left_side, right_side, (((0,), (0,)), ((), ())), preferred_element_type=jnp.float32
    )


def dot_cols(left_side, right_side):
    return lax.dot_general(
        left_side, right_side, (((1,), (1,)), ((), ())), preferred_element_type=jnp.float32
    )


def dot(left_side, right_side):
    return jnp.dot(left_side, right_side, preferred_element_type=jnp.float32)


def gather_tokens(rows):
    return lax.all_gather(rows, "tensor", axis=0, tiled=True)


def scatter_tokens(partial):
    return lax.psum_scatter(
        partial.astype(LOW), "tensor", scatter_dimension=0, tiled=True
    ).astype(jnp.float32)


def norm_forward(values, gain_row, shift_row):
    center = values - jnp.mean(values, axis=-1, keepdims=True)
    spread = jnp.mean(center * center, axis=-1, keepdims=True)
    inverse = lax.rsqrt(spread + NORM_EPS)
    scaled = center * inverse
    return (scaled * gain_row + shift_row, scaled, inverse)


def norm_backward(upstream, scaled, inverse, gain_row):
    weighted = upstream * gain_row
    inner_term = (
        weighted
        - jnp.mean(weighted, axis=-1, keepdims=True)
        - scaled * jnp.mean(weighted * scaled, axis=-1, keepdims=True)
    )
    return (inverse * inner_term, jnp.sum(upstream * scaled, axis=0), jnp.sum(upstream, axis=0))


def gelu_slope(values):
    return 0.5 * (1.0 + lax.erf(values * ROOT_HALF)) + values * INV_ROOT_TWOPI * jnp.exp(
        -0.5 * values * values
    )


def to_heads(rows, micro):
    parts = lax.axis_size("tensor")
    width = rows.shape[-1]
    shaped = rows.reshape(parts, micro, -1, width // HEAD_DIM, HEAD_DIM)
    shaped = shaped.transpose(1, 3, 0, 2, 4)
    return shaped.reshape(micro, width // HEAD_DIM, -1, HEAD_DIM)


def from_heads(block):
    micro, heads, count, _ = block.shape
    parts = lax.axis_size("tensor")
    shaped = block.reshape(micro, heads, parts, count // parts, HEAD_DIM)
    return shaped.transpose(2, 0, 3, 1, 4).reshape(micro * count, heads * HEAD_DIM)


def attend(queries, key_rows, value_rows, allowed):
    scores = jnp.einsum(
        "mhqe,mhke->mhqk", queries, key_rows, preferred_element_type=jnp.float32
    ) * HEAD_DIM ** (-0.5)
    scores = jnp.where(allowed, scores, MASKED)
    largest = jnp.max(scores, axis=-1, keepdims=True)
    raised = jnp.exp(scores - largest)
    probs = raised / jnp.sum(raised, axis=-1, keepdims=True)
    context = jnp.einsum(
        "mhqk,mhke->mhqe", probs.astype(LOW), value_rows, preferred_element_type=jnp.float32
    )
    return (context.astype(LOW), probs)


def attend_back(queries, key_rows, value_rows, probs, grad_context):
    scale = HEAD_DIM ** (-0.5)
    grad_probs = jnp.einsum(
        "mhqe,mhke->mhqk", grad_context, value_rows, preferred_element_type=jnp.float32
    )
    inner_term = jnp.sum(probs * grad_probs, axis=-1, keepdims=True)
    grad_scores = (probs * (grad_probs - inner_term)).astype(LOW)
    grad_query = (
        jnp.einsum("mhqk,mhke->mhqe", grad_scores, key_rows, preferred_element_type=jnp.float32)
        * scale
    )
    grad_keys = (
        jnp.einsum("mhqk,mhqe->mhke", grad_scores, queries, preferred_element_type=jnp.float32)
        * scale
    )
    grad_values = jnp.einsum(
        "mhqk,mhqe->mhke", probs.astype(LOW), grad_context, preferred_element_type=jnp.float32
    )
    return [from_heads(member.astype(LOW)) for member in (grad_query, grad_keys, grad_values)]


def layer_forward(current, micro, allowed, weights, vectors):
    w_qkv, w_o, w_in, w_out = weights
    gains, biases, query_bias, value_bias, local_hidden_bias = vectors
    gathered = gather_tokens(current)
    width = query_bias.shape[0]
    projected = dot(gathered, w_qkv)
    queries = to_heads((projected[:, :width] + query_bias).astype(LOW), micro)
    key_rows = to_heads(projected[:, width : 2 * width].astype(LOW), micro)
    value_rows = to_heads((projected[:, 2 * width :] + value_bias).astype(LOW), micro)
    context, probs = attend(queries, key_rows, value_rows, allowed)
    context = from_heads(context)
    mixed_rows = scatter_tokens(dot(context, w_o))
    normed, scaled_one, inverse_one = norm_forward(
        current.astype(jnp.float32) + mixed_rows + biases[2], gains[0], biases[3]
    )
    spread_rows = gather_tokens(normed.astype(LOW))
    hidden = dot(spread_rows, w_in) + local_hidden_bias
    active = jax.nn.gelu(hidden, approximate=False).astype(LOW)
    branch = scatter_tokens(dot(active, w_out))
    final_rows, scaled_two, inverse_two = norm_forward(
        normed + branch + biases[4], gains[1], biases[5]
    )
    kept = (
        gathered, queries, key_rows, value_rows, probs, context, scaled_one, inverse_one,
        spread_rows, hidden, active, scaled_two, inverse_two,
    )
    return (final_rows.astype(LOW), kept)


def layer_backward(upstream, kept, weights, gains):
    (
        gathered, queries, key_rows, value_rows, probs, context, scaled_one, inverse_one,
        spread_rows, hidden, active, scaled_two, inverse_two,
    ) = kept
    micro = queries.shape[0]
    w_qkv, w_o, w_in, w_out = weights
    grad_second, gain_two, shift_two = norm_backward(upstream, scaled_two, inverse_two, gains[1])
    grad_feed = gather_tokens(grad_second.astype(LOW))
    grad_active = dot_cols(grad_feed, w_out)
    grad_hidden = (grad_active * gelu_slope(hidden)).astype(LOW)
    part = scatter_tokens(dot_cols(grad_hidden, w_in))
    grad_w_out = dot_rows(active, grad_feed).astype(LOW)
    grad_w_in = dot_rows(spread_rows, grad_hidden).astype(LOW)
    grad_normed = grad_second + part
    grad_first, gain_one, shift_one = norm_backward(grad_normed, scaled_one, inverse_one, gains[0])
    grad_mix = gather_tokens(grad_first.astype(LOW))
    grad_context = to_heads(dot_cols(grad_mix, w_o).astype(LOW), micro)
    pieces = attend_back(queries, key_rows, value_rows, probs, grad_context)
    grad_project = jnp.concatenate(pieces, axis=1)
    part = scatter_tokens(dot_cols(grad_project, w_qkv))
    grad_w_o = dot_rows(context, grad_mix).astype(LOW)
    grad_w_qkv = dot_rows(gathered, grad_project).astype(LOW)
    grad_current = grad_first + part
    width = pieces[0].shape[1]
    column_sums = jnp.sum(grad_project.astype(jnp.float32), axis=0)
    row_grads = jnp.stack(
        [
            gain_one, gain_two, jnp.sum(grad_first, axis=0), shift_one,
            jnp.sum(grad_second, axis=0), shift_two,
        ]
    )
    hidden_grads = jnp.sum(grad_hidden.astype(jnp.float32), axis=0)
    return (
        grad_current.astype(LOW),
        (grad_w_qkv, grad_w_o, grad_w_in, grad_w_out),
        (row_grads, column_sums[:width], column_sums[2 * width :], hidden_grads),
    )


def body(inputs, segments, cotangent, w_qkv, w_o, w_in, w_out, ln_gains, model_biases, hidden_bias):
    half = lax.axis_index("pipe")
    first = half == 0
    column = lax.axis_index("tensor")
    sections = lax.axis_size("pipe")
    parts = lax.axis_size("dp")
    columns = lax.axis_size("tensor")
    micro = inputs.shape[0] // sections
    row_count = inputs.shape[1]
    model_width = inputs.shape[2]
    width = w_qkv.shape[-1]
    hidden_local = w_in.shape[-1]
    hidden_width = hidden_bias.shape[-1]
    block = w_qkv.shape[1]

    shards = (
        w_qkv[0].reshape(block, 3 * width), w_o[0].T, w_in[0], w_out[0].T
    )
    stacks = [
        lax.all_gather(shard, ("pipe", "dp"), axis=0, tiled=True).reshape(
            sections, parts * shard.shape[0], shard.shape[1]
        )
        for shard in shards
    ]
    gains_all = lax.all_gather(ln_gains[0], "pipe")
    biases_all = lax.all_gather(model_biases[0], "pipe")
    hidden_all = lax.all_gather(hidden_bias[0], "pipe")

    def own_slice(array, size, dim):
        return lax.dynamic_slice_in_dim(array, column * size, size, dim)

    def own_micro(array):
        return lax.dynamic_slice_in_dim(array, half * micro, micro, 0)

    labels = own_micro(segments)
    allowed = (labels[:, :, None] == labels[:, None, :])[:, None]
    weights, vectors = [], []
    for layer in range(sections):
        weights.append(
            (stacks[0][layer], stacks[1][layer].T, stacks[2][layer], stacks[3][layer].T)
        )
        biases = biases_all[layer]
        vectors.append(
            (
                gains_all[layer], biases, own_slice(biases[0], width, 0),
                own_slice(biases[1], width, 0), own_slice(hidden_all[layer], hidden_local, 0),
            )
        )
    current = own_micro(inputs).reshape(micro * row_count, model_width)
    outs, kept_list = [], []
    for layer in range(sections):
        current, kept = layer_forward(current, micro, allowed, weights[layer], vectors[layer])
        outs.append(current)
        kept_list.append(kept)
    upstream = own_micro(cotangent).reshape(micro * row_count, model_width)
    grads = [None] * sections
    totals = [None] * sections
    packs = [None] * sections
    zero = jnp.zeros((), jnp.int32)
    for layer in reversed(range(sections)):
        upstream, weight_grads, vector_grads = layer_backward(
            upstream.astype(jnp.float32), kept_list[layer], weights[layer], vectors[layer][0]
        )
        grads[layer] = upstream
        shaped = (
            weight_grads[0].reshape(parts, block, 3 * width),
            weight_grads[1].reshape(width, parts, model_width // parts),
            weight_grads[2].reshape(parts, block, hidden_local),
            weight_grads[3].reshape(hidden_local, parts, model_width // parts),
        )
        totals[layer] = [
            halve_sum(member, "dp", dim, LOW) for member, dim in zip(shaped, (0, 1, 0, 1))
        ]
        row_grads, query_grad, value_grad, hidden_grads = vector_grads
        placed = lax.dynamic_update_slice(
            jnp.zeros((2, model_width), jnp.float32),
            jnp.stack([query_grad, value_grad]),
            (zero, column * width),
        )
        hidden_full = lax.dynamic_update_slice(
            jnp.zeros((hidden_width,), jnp.float32), hidden_grads, (column * hidden_local,)
        )
        blocks = parts * columns
        packs[layer] = jnp.concatenate(
            [
                jnp.concatenate([row_grads[:2], placed, row_grads[2:]], axis=0)
                .reshape(8, blocks, model_width // blocks)
                .transpose(1, 0, 2)
                .reshape(blocks, -1),
                hidden_full.reshape(blocks, hidden_width // blocks),
            ],
            axis=1,
        )

    def exchanged(pair):
        return jnp.where(first, pair[0], pair[1]), swapped(jnp.where(first, pair[1], pair[0]), "pipe", 1)

    summed = []
    for index in range(4):
        own, came = exchanged([totals[0][index], totals[1][index]])
        summed.append(own.astype(jnp.float32) + came.astype(jnp.float32))
    own, came = exchanged(packs)
    pack = (own + came).reshape(parts, columns, -1)
    pack = halve_sum(pack, "dp", 0, jnp.float32)
    pack = halve_sum(pack, "tensor", 0, jnp.float32)
    rows_each = model_width // (parts * columns)
    vector_part = pack[: 8 * rows_each].reshape(8, rows_each)

    def both_halves(pair):
        own, came = exchanged(pair)
        shape = (micro, row_count, model_width)
        own, came = own.reshape(shape), came.reshape(shape)
        return jnp.concatenate(
            [jnp.where(first, own, came), jnp.where(first, came, own)], axis=0
        )[None]

    return (
        both_halves(outs),
        both_halves(grads),
        summed[0].reshape(1, block, 3, width),
        summed[1][None],
        summed[2][None],
        summed[3][None],
        vector_part[:2][None],
        vector_part[2:][None],
        pack[8 * rows_each :][None],
    )


def solution(mesh):
    return jax.shard_map(
        body,
        mesh=mesh,
        in_specs=(
            P(None, ("dp", "tensor"), None),
            P(None, "dp"),
            P(None, ("dp", "tensor"), None),
            P("pipe", "dp", None, "tensor"),
            P("pipe", "tensor", "dp"),
            P("pipe", "dp", "tensor"),
            P("pipe", "tensor", "dp"),
            P("pipe", None, None),
            P("pipe", None, None),
            P("pipe", None),
        ),
        out_specs=(
            P("pipe", None, ("dp", "tensor"), None),
            P("pipe", None, ("dp", "tensor"), None),
            P("pipe", "dp", None, "tensor"),
            P("pipe", "tensor", "dp"),
            P("pipe", "dp", "tensor"),
            P("pipe", "tensor", "dp"),
            P("pipe", None, ("dp", "tensor")),
            P("pipe", None, ("dp", "tensor")),
            P("pipe", ("dp", "tensor")),
        ),
        check_vma=False,
    )
```

```python
import jax
import jax.numpy as jnp
from jax import lax
from jax.sharding import PartitionSpec as P

HEAD_DIM = 64
NORM_EPS = 1e-12
MASKED = -1000000000.0
ROOT_HALF = 0.7071067811865476
INV_ROOT_TWOPI = 0.3989422804014327
LOW = jnp.bfloat16


def swapped(block, axis, bit):
    size = lax.axis_size(axis)
    return lax.ppermute(block, axis, [(i, i ^ bit) for i in range(size)])


def halve_sum(stack, axis, dim, kind):
    size = lax.axis_size(axis)
    own = lax.axis_index(axis)
    bit = 1
    while bit < size:
        count = stack.shape[dim]
        split = stack.reshape(stack.shape[:dim] + (count // 2, 2) + stack.shape[dim + 1 :])
        side = (own // bit) % 2
        kept = lax.dynamic_index_in_dim(split, side, dim + 1, keepdims=False)
        given = lax.dynamic_index_in_dim(split, 1 - side, dim + 1, keepdims=False)
        came = swapped(given, axis, bit)
        stack = (kept.astype(jnp.float32) + came.astype(jnp.float32)).astype(kind)
        bit *= 2
    return lax.squeeze(stack, (dim,))


def dot_rows(left_side, right_side):
    return lax.dot_general(
        left_side, right_side, (((0,), (0,)), ((), ())), preferred_element_type=jnp.float32
    )


def dot_cols(left_side, right_side):
    return lax.dot_general(
        left_side, right_side, (((1,), (1,)), ((), ())), preferred_element_type=jnp.float32
    )


def dot(left_side, right_side):
    return jnp.dot(left_side, right_side, preferred_element_type=jnp.float32)


class Columns:
    def gather(self, rows):
        return lax.all_gather(rows, "tensor", axis=0, tiled=True)

    def scatter(self, partial):
        return lax.psum_scatter(
            partial.astype(LOW), "tensor", scatter_dimension=0, tiled=True
        ).astype(jnp.float32)

    def to_heads(self, rows, micro):
        parts = lax.axis_size("tensor")
        width = rows.shape[-1]
        shaped = rows.reshape(parts, micro, -1, width // HEAD_DIM, HEAD_DIM)
        shaped = shaped.transpose(1, 3, 0, 2, 4)
        return shaped.reshape(micro, width // HEAD_DIM, -1, HEAD_DIM)

    def from_heads(self, block):
        micro, heads, count, _ = block.shape
        parts = lax.axis_size("tensor")
        shaped = block.reshape(micro, heads, parts, count // parts, HEAD_DIM)
        return shaped.transpose(2, 0, 3, 1, 4).reshape(micro * count, heads * HEAD_DIM)


class Quads:
    def gather(self, rows):
        near = jnp.concatenate([rows, swapped(rows, "tensor", 1)], axis=0)
        return jnp.concatenate([near, swapped(near, "dp", 1)], axis=0)

    def scatter(self, partial):
        low = partial.astype(LOW)
        count = low.shape[0] // 2
        near = partial[:count] + swapped(low[count:], "dp", 1).astype(jnp.float32)
        count = count // 2
        came = swapped(near[count:].astype(LOW), "tensor", 1)
        return near[:count] + came.astype(jnp.float32)

    def to_heads(self, rows, micro):
        width = rows.shape[-1]
        shaped = rows.reshape(micro, -1, width // HEAD_DIM, HEAD_DIM)
        return shaped.transpose(0, 2, 1, 3)

    def from_heads(self, block):
        micro, heads, count, _ = block.shape
        return block.transpose(0, 2, 1, 3).reshape(micro * count, heads * HEAD_DIM)


def norm_forward(values, gain_row, shift_row):
    center = values - jnp.mean(values, axis=-1, keepdims=True)
    spread = jnp.mean(center * center, axis=-1, keepdims=True)
    inverse = lax.rsqrt(spread + NORM_EPS)
    scaled = center * inverse
    return (scaled * gain_row + shift_row, scaled, inverse)


def norm_backward(upstream, scaled, inverse, gain_row):
    weighted = upstream * gain_row
    inner_term = (
        weighted
        - jnp.mean(weighted, axis=-1, keepdims=True)
        - scaled * jnp.mean(weighted * scaled, axis=-1, keepdims=True)
    )
    return (inverse * inner_term, jnp.sum(upstream * scaled, axis=0), jnp.sum(upstream, axis=0))


def gelu_slope(values):
    return 0.5 * (1.0 + lax.erf(values * ROOT_HALF)) + values * INV_ROOT_TWOPI * jnp.exp(
        -0.5 * values * values
    )


def attend(queries, key_rows, value_rows, allowed):
    scores = jnp.einsum(
        "mhqe,mhke->mhqk", queries, key_rows, preferred_element_type=jnp.float32
    ) * HEAD_DIM ** (-0.5)
    scores = jnp.where(allowed, scores, MASKED)
    largest = jnp.max(scores, axis=-1, keepdims=True)
    raised = jnp.exp(scores - largest)
    probs = raised / jnp.sum(raised, axis=-1, keepdims=True)
    context = jnp.einsum(
        "mhqk,mhke->mhqe", probs.astype(LOW), value_rows, preferred_element_type=jnp.float32
    )
    return (context.astype(LOW), probs)


def attend_back(queries, key_rows, value_rows, probs, grad_context):
    scale = HEAD_DIM ** (-0.5)
    grad_probs = jnp.einsum(
        "mhqe,mhke->mhqk", grad_context, value_rows, preferred_element_type=jnp.float32
    )
    inner_term = jnp.sum(probs * grad_probs, axis=-1, keepdims=True)
    grad_scores = (probs * (grad_probs - inner_term)).astype(LOW)
    grad_query = (
        jnp.einsum("mhqk,mhke->mhqe", grad_scores, key_rows, preferred_element_type=jnp.float32)
        * scale
    )
    grad_keys = (
        jnp.einsum("mhqk,mhqe->mhke", grad_scores, queries, preferred_element_type=jnp.float32)
        * scale
    )
    grad_values = jnp.einsum(
        "mhqk,mhqe->mhke", probs.astype(LOW), grad_context, preferred_element_type=jnp.float32
    )
    return [member.astype(LOW) for member in (grad_query, grad_keys, grad_values)]


def layer_forward(move, current, micro, allowed, weights, vectors):
    w_qkv, w_o, w_in, w_out = weights
    gains, biases, query_bias, value_bias, local_hidden_bias = vectors
    gathered = move.gather(current)
    width = query_bias.shape[0]
    projected = dot(gathered, w_qkv)
    queries = move.to_heads((projected[:, :width] + query_bias).astype(LOW), micro)
    key_rows = move.to_heads(projected[:, width : 2 * width].astype(LOW), micro)
    value_rows = move.to_heads((projected[:, 2 * width :] + value_bias).astype(LOW), micro)
    context, probs = attend(queries, key_rows, value_rows, allowed)
    context = move.from_heads(context)
    mixed_rows = move.scatter(dot_cols(context, w_o))
    normed, scaled_one, inverse_one = norm_forward(
        current.astype(jnp.float32) + mixed_rows + biases[2], gains[0], biases[3]
    )
    spread_rows = move.gather(normed.astype(LOW))
    hidden = dot(spread_rows, w_in) + local_hidden_bias
    active = jax.nn.gelu(hidden, approximate=False).astype(LOW)
    branch = move.scatter(dot_cols(active, w_out))
    final_rows, scaled_two, inverse_two = norm_forward(
        normed + branch + biases[4], gains[1], biases[5]
    )
    kept = (
        gathered, queries, key_rows, value_rows, probs, context, scaled_one, inverse_one,
        spread_rows, hidden, active, scaled_two, inverse_two,
    )
    return (final_rows.astype(LOW), kept)


def layer_backward(move, upstream, kept, weights, gains):
    (
        gathered, queries, key_rows, value_rows, probs, context, scaled_one, inverse_one,
        spread_rows, hidden, active, scaled_two, inverse_two,
    ) = kept
    micro = queries.shape[0]
    w_qkv, w_o, w_in, w_out = weights
    grad_second, gain_two, shift_two = norm_backward(upstream, scaled_two, inverse_two, gains[1])
    grad_feed = move.gather(grad_second.astype(LOW))
    grad_active = dot(grad_feed, w_out)
    grad_hidden = (grad_active * gelu_slope(hidden)).astype(LOW)
    part = move.scatter(dot_cols(grad_hidden, w_in))
    grad_w_out = dot_rows(grad_feed, active).astype(LOW)
    grad_w_in = dot_rows(spread_rows, grad_hidden).astype(LOW)
    grad_normed = grad_second + part
    grad_first, gain_one, shift_one = norm_backward(grad_normed, scaled_one, inverse_one, gains[0])
    grad_mix = move.gather(grad_first.astype(LOW))
    grad_context = move.to_heads(dot(grad_mix, w_o).astype(LOW), micro)
    pieces = attend_back(queries, key_rows, value_rows, probs, grad_context)
    pieces = [move.from_heads(member) for member in pieces]
    grad_project = jnp.concatenate(pieces, axis=1)
    part = move.scatter(dot_cols(grad_project, w_qkv))
    grad_w_o = dot_rows(grad_mix, context).astype(LOW)
    grad_w_qkv = dot_rows(gathered, grad_project).astype(LOW)
    grad_current = grad_first + part
    width = pieces[0].shape[1]
    column_sums = jnp.sum(grad_project.astype(jnp.float32), axis=0)
    row_grads = jnp.stack(
        [
            gain_one, gain_two, jnp.sum(grad_first, axis=0), shift_one,
            jnp.sum(grad_second, axis=0), shift_two,
        ]
    )
    hidden_grads = jnp.sum(grad_hidden.astype(jnp.float32), axis=0)
    return (
        grad_current.astype(LOW),
        (grad_w_qkv, grad_w_o, grad_w_in, grad_w_out),
        (row_grads, column_sums[:width], column_sums[2 * width :], hidden_grads),
    )


def flipped(array, axis, when):
    return jnp.where(when, jnp.flip(array, axis), array)


def pick(array, index):
    return lax.dynamic_index_in_dim(array, index, 0, keepdims=False)


def summed_pair(one, two, kind):
    return (one.astype(jnp.float32) + two.astype(jnp.float32)).astype(kind)


def one_way(block, source):
    return lax.ppermute(block, "pipe", [(source, 1 - source)])


class General:
    move = Columns()

    def __init__(self, micro, row_count):
        self.micro, self.row_count = micro, row_count
        self.half = lax.axis_index("pipe")
        self.column = lax.axis_index("tensor")

    def mine(self, array):
        return lax.dynamic_slice_in_dim(array, self.half * self.micro, self.micro, 0)

    def labels(self, segments):
        return self.mine(segments)

    def rows_in(self, array):
        return self.mine(array).reshape(self.micro * self.row_count, -1)

    def rows_out(self, rows):
        return rows.reshape(self.micro, self.row_count, -1)

    def weights(self, shard):
        full = lax.all_gather(shard, ("pipe", "dp"), axis=0, tiled=True)
        return full.reshape(2, -1, shard.shape[1])

    def reduced(self, layer, grad):
        parts = lax.axis_size("dp")
        total = halve_sum(grad.reshape(parts, -1, grad.shape[1]), "dp", 0, LOW)
        return summed_pair(total, one_way(total, 1 - layer), LOW)

    def finished(self, totals):
        return jnp.where(self.half == 0, totals[0], totals[1]).astype(jnp.float32)


class Paired(General):
    move = Quads()

    def __init__(self, micro, row_count):
        super().__init__(micro, row_count)
        place = lax.axis_index("dp")
        self.core, self.side = place % 2, place // 2
        self.near, self.group = self.column % 2, self.column // 2
        self.home = self.group == self.core
        self.column = self.near + 2 * self.core

    def labels(self, segments):
        own = pick(segments, self.half * self.micro + self.group)
        both = jnp.stack([own, swapped(own, "dp", 1)]).reshape(2, 2, 2, -1)
        both = flipped(flipped(both, 1, self.group == 1), 2, self.near == 1)
        return both.transpose(0, 2, 1, 3).reshape(2, -1)

    def rows_in(self, array):
        kept = pick(array, self.half * self.micro + self.group)
        given = pick(array, self.half * self.micro + 1 - self.group)
        return jnp.concatenate([kept, swapped(given, "tensor", 2)], axis=0)

    def rows_out(self, rows):
        own, away = rows[: self.row_count], rows[self.row_count :]
        return flipped(jnp.stack([own, swapped(away, "tensor", 2)]), 0, self.group == 1)

    def weights(self, shard):
        far = swapped(shard, "tensor", 2)
        want = jnp.where(self.home, shard, far)
        given = jnp.where(self.home, far, shard)
        pair = jnp.stack([want, swapped(given, "dp", 1)])
        other = swapped(pair, "pipe", 1)
        layers = []
        for layer in range(2):
            part = jnp.where(self.half == layer, pair, other)
            full = jnp.stack([part, swapped(part, "dp", 2)])
            full = flipped(flipped(full, 1, self.core == 1), 0, self.side == 1)
            layers.append(full.reshape(-1, shard.shape[1]))
        return layers

    def reduced(self, layer, grad):
        split = grad.reshape(2, 2, -1, grad.shape[1])
        came = swapped(pick(split, 1 - self.side), "dp", 2)
        total = summed_pair(pick(split, self.side), came, LOW)
        return summed_pair(total, one_way(total, 1 - layer), LOW)

    def finished(self, totals):
        mine = jnp.where(self.half == 0, totals[0], totals[1])
        kept = pick(mine, self.core)
        came = swapped(pick(mine, 1 - self.core), "dp", 1)
        own = jnp.where(self.home, kept, came)
        away = jnp.where(self.home, came, kept)
        return summed_pair(own, swapped(away, "tensor", 2), jnp.float32)


def body(inputs, segments, cotangent, w_qkv, w_o, w_in, w_out, ln_gains, model_biases, hidden_bias):
    sections = lax.axis_size("pipe")
    parts = lax.axis_size("dp")
    columns = lax.axis_size("tensor")
    micro = inputs.shape[0] // sections
    row_count = inputs.shape[1]
    model_width = inputs.shape[2]
    width = w_qkv.shape[-1]
    hidden_local = w_in.shape[-1]
    hidden_width = hidden_bias.shape[-1]
    block = w_qkv.shape[1]
    paired = parts == 4 and columns == 4 and micro == 2
    plan = (Paired if paired else General)(micro, row_count)
    first = plan.half == 0
    column = plan.column

    vector_own = jnp.concatenate([ln_gains[0].reshape(-1), model_biases[0].reshape(-1), hidden_bias[0]])
    vector_other = swapped(vector_own, "pipe", 1)
    labels = plan.labels(segments)
    current = plan.rows_in(inputs)
    stacks = [
        plan.weights(w_qkv[0].reshape(block, 3 * width)),
        plan.weights(w_o[0].T),
        plan.weights(w_in[0]),
        plan.weights(w_out[0].T),
    ]

    def own_slice(array, size):
        return lax.dynamic_slice_in_dim(array, column * size, size, 0)

    allowed = (labels[:, :, None] == labels[:, None, :])[:, None]
    weights, vectors = [], []
    for layer in range(sections):
        weights.append(tuple(stack[layer] for stack in stacks))
        flat = jnp.where(plan.half == layer, vector_own, vector_other)
        gains = flat[: 2 * model_width].reshape(2, model_width)
        biases = flat[2 * model_width : 8 * model_width].reshape(6, model_width)
        vectors.append(
            (
                gains, biases, own_slice(biases[0], width), own_slice(biases[1], width),
                own_slice(flat[8 * model_width :], hidden_local),
            )
        )
    outs, kept_list = [], []
    for layer in range(sections):
        current, kept = layer_forward(
            plan.move, current, micro, allowed, weights[layer], vectors[layer]
        )
        outs.append(plan.rows_out(current))
        kept_list.append(kept)
    upstream = plan.rows_in(cotangent)
    grads = [None] * sections
    totals = [None] * sections
    packs = [None] * sections
    zero = jnp.zeros((), jnp.int32)
    blocks = parts * columns
    for layer in reversed(range(sections)):
        upstream, weight_grads, vector_grads = layer_backward(
            plan.move, upstream.astype(jnp.float32), kept_list[layer], weights[layer], vectors[layer][0]
        )
        grads[layer] = plan.rows_out(upstream)
        totals[layer] = [plan.reduced(layer, member) for member in weight_grads]
        row_grads, query_grad, value_grad, hidden_grads = vector_grads
        placed = lax.dynamic_update_slice(
            jnp.zeros((2, model_width), jnp.float32),
            jnp.stack([query_grad, value_grad]),
            (zero, column * width),
        )
        hidden_full = lax.dynamic_update_slice(
            jnp.zeros((hidden_width,), jnp.float32), hidden_grads, (column * hidden_local,)
        )
        packs[layer] = jnp.concatenate(
            [
                jnp.concatenate([row_grads[:2], placed, row_grads[2:]], axis=0)
                .reshape(8, blocks, model_width // blocks)
                .transpose(1, 0, 2)
                .reshape(blocks, -1),
                hidden_full.reshape(blocks, hidden_width // blocks),
            ],
            axis=1,
        )
    summed = [plan.finished([totals[0][index], totals[1][index]]) for index in range(4)]

    def exchanged(pair):
        return jnp.where(first, pair[0], pair[1]), swapped(jnp.where(first, pair[1], pair[0]), "pipe", 1)

    own, came = exchanged(packs)
    pack = (own + came).reshape(parts, columns, -1)
    pack = halve_sum(pack, "dp", 0, jnp.float32)
    pack = halve_sum(pack, "tensor", 0, jnp.float32)
    rows_each = model_width // blocks
    vector_part = pack[: 8 * rows_each].reshape(8, rows_each)

    def both_halves(pair):
        own, came = exchanged(pair)
        return jnp.concatenate(
            [jnp.where(first, own, came), jnp.where(first, came, own)], axis=0
        )[None]

    return (
        both_halves(outs),
        both_halves(grads),
        summed[0].reshape(1, block, 3, width),
        summed[1].T[None],
        summed[2][None],
        summed[3].T[None],
        vector_part[:2][None],
        vector_part[2:][None],
        pack[8 * rows_each :][None],
    )


def solution(mesh):
    return jax.shard_map(
        body,
        mesh=mesh,
        in_specs=(
            P(None, ("dp", "tensor"), None),
            P(None, "dp"),
            P(None, ("dp", "tensor"), None),
            P("pipe", "dp", None, "tensor"),
            P("pipe", "tensor", "dp"),
            P("pipe", "dp", "tensor"),
            P("pipe", "tensor", "dp"),
            P("pipe", None, None),
            P("pipe", None, None),
            P("pipe", None),
        ),
        out_specs=(
            P("pipe", None, ("dp", "tensor"), None),
            P("pipe", None, ("dp", "tensor"), None),
            P("pipe", "dp", None, "tensor"),
            P("pipe", "tensor", "dp"),
            P("pipe", "dp", "tensor"),
            P("pipe", "tensor", "dp"),
            P("pipe", None, ("dp", "tensor")),
            P("pipe", None, ("dp", "tensor")),
            P("pipe", ("dp", "tensor")),
        ),
        check_vma=False,
    )
```
